32 devices in a mesh: groups: 2 (over x), seq: 16 (over z, y, core).
Axes of the slice: x: 2, y: 2, z: 4, core: 2. Of those that a mesh axis runs over, the one named last changes fastest.
Arguments:
- queries: bfloat16 [32, 384, 1280], P(('groups', 'seq')), parts along dimension 0, may hold values from -11 to 11
- key_vectors: bfloat16 [32, 384, 1280], P(('groups', 'seq')), parts along dimension 0, may hold values from -11 to 11
- value_vectors: bfloat16 [32, 384, 1280], P(('groups', 'seq')), parts along dimension 0, may hold values from -5 to 5
- out_grad: bfloat16 [32, 384, 1280], P(('groups', 'seq')), parts along dimension 0, may hold values from -5 to 5
- tile_lists: int32 [16, 5], P('groups'), parts along dimension 0, may hold values from -1 to 7, as said below
Outputs:
- attended: bfloat16 [32, 384, 1280], P(('groups', 'seq')), parts along dimension 0
- query_grad: bfloat16 [32, 384, 1280], P(('groups', 'seq')), parts along dimension 0
- key_grad: bfloat16 [32, 384, 1280], P(('groups', 'seq')), parts along dimension 0
- value_grad: bfloat16 [32, 384, 1280], P(('groups', 'seq')), parts along dimension 0
The draws below stay inside these ranges and needn't reach their ends.
There are 2 independent parts, one for each index of `groups`. The reference program is written for one: setup_inputs(seed, part) draws one part's arguments, and reference() takes and returns one part's arrays. A program takes and returns all parts, laid end to end along the dimension named above; each array names one. Nothing has to cross between parts.
Inputs may be any that keep to these rules, and one draw needn't show every extreme that they name: `tile_lists`: row s lists in ascending order tile s itself, every neighbour of s along the width inside the grid, and some of its neighbours along height and time, then -1 in the unused slots.
All inputs are finite; a program needn't handle non-finite values.
Results may differ from the reference program's by a relative error of at most 0.023.
Values may be sent and summed in bfloat16 or wider, within the bound.
A program may use at most 192 MiB of HBM per device.

```python
import jax
import jax.numpy as jnp
from jax import lax

HEADS = 20
HD = 128
TOK = 384
TILES = 8
ROWS = 16
HALF_W = 1280


def drawn_pair(key):
    shape = (ROWS, TOK, HEADS // 2 * HD)
    query_key, key_key = jax.random.split(jax.random.fold_in(key, 7), 2)
    query_draw = 1.4 * jax.random.truncated_normal(query_key, -4.0, 4.0, shape, jnp.float32)
    key_draw = 1.4 * jax.random.truncated_normal(key_key, -4.0, 4.0, shape, jnp.float32)
    return (query_draw, key_draw)


def draw_queries(key, part):
    return drawn_pair(key)[0].astype(jnp.bfloat16)


def draw_key_vectors(key, part):
    return drawn_pair(key)[1].astype(jnp.bfloat16)


def draw_tile_lists(key, part):
    grid_w = TILES // 4
    tile_slot = jnp.arange(TILES, dtype=jnp.int32)
    column = tile_slot // 4
    tile_ids = jnp.stack([tile_slot, tile_slot - 4, tile_slot + 4, jnp.bitwise_xor(tile_slot, 1), jnp.bitwise_xor(tile_slot, 2)], axis=1)
    inside = jnp.stack([tile_slot >= 0, column > 0, column < grid_w - 1, tile_slot >= 0, tile_slot >= 0], axis=1)
    keeping = jax.random.randint(jax.random.fold_in(key, 3), (TILES, 5), 0, 4) > 0
    keeping = keeping.at[:, 0].set(True)
    keeping = keeping.at[:, 1].set(True)
    keeping = keeping.at[:, 2].set(True)
    entries = jnp.where(inside & keeping, tile_ids, TILES)
    entries = jnp.sort(entries, axis=1)
    return jnp.where(entries >= TILES, -1, entries).astype(jnp.int32)


def block_scale(key, dims, cuts, low, high):
    level, own = 1.0, jax.random.fold_in(key, 6)
    for dim, parts in cuts:
        heights = jnp.exp(jax.random.uniform(jax.random.fold_in(own, dim), (parts,), jnp.float32, low / len(cuts), high / len(cuts)))
        level = level * jnp.repeat(heights, dims[dim] // parts).reshape([-1 if axis == dim else 1 for axis in range(len(dims))])
    return level


def gaussian(key, shape, spread, bound, pieces=(), held_as=jnp.bfloat16):
    result = spread * jax.random.normal(key, shape, jnp.float32)
    if pieces:
        result = result * block_scale(key, shape, pieces, -0.22, 0.18)
    return jnp.clip(result, -bound, bound).astype(held_as)


def setup_inputs(seed: int = 0, part: int = 0) -> dict:
    streams_of = jax.random.split(jax.random.key(seed), 6)
    part_keys = jax.random.split(jax.random.fold_in(streams_of[5], part), 6)
    queries = draw_queries(jax.random.fold_in(jax.random.fold_in(streams_of[5], part), 71), part)
    key_vectors = draw_key_vectors(jax.random.fold_in(jax.random.fold_in(streams_of[5], part), 71), part)
    value_vectors = gaussian(part_keys[2], (ROWS, TOK, HALF_W), 2.0, 5.0, ((0, 16),))
    out_grad = gaussian(part_keys[3], (ROWS, TOK, HALF_W), 1.0, 5.0, ((0, 16),))
    tile_lists = draw_tile_lists(jax.random.fold_in(jax.random.fold_in(streams_of[5], part), 71), part)
    return dict(queries=queries, key_vectors=key_vectors, value_vectors=value_vectors, out_grad=out_grad, tile_lists=tile_lists)


def neighbour_tiles(tile_slot):
    grid_w = TILES // 4
    column = tile_slot // 4
    tile_ids = jnp.stack([tile_slot, tile_slot - 4, tile_slot + 4, jnp.bitwise_xor(tile_slot, 1), jnp.bitwise_xor(tile_slot, 2)]).astype(jnp.int32)
    inside = jnp.stack([column >= 0, column > 0, column < grid_w - 1, column >= 0, column >= 0])
    return jnp.clip(tile_ids, 0, TILES - 1).astype(jnp.int32), inside


def reference(queries, key_vectors, value_vectors, out_grad, tile_lists):
    score_scale = HD ** -0.5
    head_count = HEADS // 2

    def shaped(rows):
        return rows.astype(jnp.float32).reshape(rows.shape[:-1] + (head_count, HD))

    def query_pass(row_index):
        tile_slot = row_index // 2
        half_index = row_index % 2
        tile_ids, inside = neighbour_tiles(tile_slot)
        listed = tile_lists[tile_slot]
        in_use = inside & jnp.any(listed[None, :] == tile_ids[:, None], axis=1)
        key_index = (2 * tile_ids + half_index).astype(jnp.int32)
        query_row = shaped(queries[row_index])
        grad_row = shaped(out_grad[row_index])
        near_keys = shaped(key_vectors[key_index])
        near_values = shaped(value_vectors[key_index])
        scores = jnp.einsum("qhd,ckhd->hqck", query_row, near_keys) * score_scale
        scores = jnp.where(in_use[None, None, :, None], scores, -jnp.inf)
        row_top = jnp.max(scores, axis=(2, 3))
        log_total = row_top + jnp.log(jnp.sum(jnp.exp(scores - row_top[:, :, None, None]), axis=(2, 3)))
        chance = jnp.exp(scores - log_total[:, :, None, None])
        rounded = lax.optimization_barrier(chance.astype(jnp.bfloat16)).astype(jnp.float32)
        attended = jnp.einsum("hqck,ckhd->qhd", rounded, near_values).reshape(TOK, HALF_W).astype(jnp.bfloat16)
        attended_wide = lax.optimization_barrier(attended).astype(jnp.float32).reshape(TOK, head_count, HD)
        delta_rows = jnp.sum(grad_row * attended_wide, axis=2).T
        pressure = jnp.einsum("qhd,ckhd->hqck", grad_row, near_values)
        score_grad = lax.optimization_barrier((chance * (pressure - delta_rows[:, :, None, None])).astype(jnp.bfloat16)).astype(jnp.float32)
        query_grad = (score_scale * jnp.einsum("hqck,ckhd->qhd", score_grad, near_keys)).reshape(TOK, HALF_W).astype(jnp.bfloat16)
        return attended, query_grad, log_total, delta_rows

    attended, query_grad, log_totals, delta_all = lax.map(query_pass, jnp.arange(ROWS, dtype=jnp.int32))

    def key_pass(row_index):
        tile_slot = row_index // 2
        half_index = row_index % 2
        tile_ids, inside = neighbour_tiles(tile_slot)
        their_lists = tile_lists[tile_ids]
        in_use = inside & jnp.any(their_lists == tile_slot, axis=1)
        query_index = (2 * tile_ids + half_index).astype(jnp.int32)
        near_queries = shaped(queries[query_index])
        near_grads = shaped(out_grad[query_index])
        near_totals = log_totals[query_index]
        near_deltas = delta_all[query_index]
        own_keys = shaped(key_vectors[row_index])
        own_values = shaped(value_vectors[row_index])
        scores = jnp.einsum("cqhd,khd->chqk", near_queries, own_keys) * score_scale
        scores = jnp.where(in_use[:, None, None, None], scores, -jnp.inf)
        chance = jnp.exp(scores - near_totals[:, :, :, None])
        rounded = lax.optimization_barrier(chance.astype(jnp.bfloat16)).astype(jnp.float32)
        pressure = jnp.einsum("cqhd,khd->chqk", near_grads, own_values)
        score_grad = lax.optimization_barrier((chance * (pressure - near_deltas[:, :, :, None])).astype(jnp.bfloat16)).astype(jnp.float32)
        value_terms = lax.optimization_barrier(jnp.einsum("chqk,cqhd->ckhd", rounded, near_grads).astype(jnp.bfloat16)).astype(jnp.float32)
        key_terms = lax.optimization_barrier((score_scale * jnp.einsum("chqk,cqhd->ckhd", score_grad, near_queries)).astype(jnp.bfloat16)).astype(jnp.float32)
        key_grad = jnp.sum(key_terms, axis=0).reshape(TOK, HALF_W).astype(jnp.bfloat16)
        value_grad = jnp.sum(value_terms, axis=0).reshape(TOK, HALF_W).astype(jnp.bfloat16)
        return key_grad, value_grad

    key_grad, value_grad = lax.map(key_pass, jnp.arange(ROWS, dtype=jnp.int32))
    return attended, query_grad, key_grad, value_grad
```

```python
import functools

import jax
import jax.numpy as jnp
from jax import lax
from jax.experimental import pallas as pl
from jax.experimental.pallas import tpu as pltpu
from jax.sharding import PartitionSpec as P

HD = 128
MESH = pl.DeviceIdType.MESH


def dot(a, b, a_dim, b_dim):
    return lax.dot_general(
        a, b, (((a_dim,), (b_dim,)), ((), ())), preferred_element_type=jnp.float32
    )


def neighbours(grid_w):
    tile = lax.axis_index("seq") // 2
    bit0 = lax.rem(tile, 2)
    bit1 = lax.rem(tile // 2, 2)
    column = tile // 4
    if grid_w == 2:
        sides = [(tile + 4 - 8 * column, None, 0)]
    else:
        sides = [(tile - 4, column > 0, 1), (tile + 4, column < grid_w - 1, 0)]
    count = len(sides)
    return sides + [
        (tile + 2 - 4 * bit1, None, count),
        (tile + 1 - 2 * bit0, None, count + 1),
    ]


def when(exists, fn):
    if exists is None:
        fn()
    else:
        pl.when(exists)(fn)


def kernel(
    grid_w, lists_ref, q_ref, k_ref, v_ref, g_ref, o_ref, dq_ref, dk_ref, dv_ref,
    kv_in, probs, term_out, term_in, kv_send, kv_recv, term_send, term_recv,
):
    me = lax.axis_index("seq")
    tile = me // 2
    core = lax.rem(me, 2)
    near = neighbours(grid_w)
    heads = q_ref.shape[2] // HD
    scale = HD ** (-0.5)

    def cols(head):
        return pl.ds(pl.multiple_of(head * HD, HD), HD)

    def kv_copy(slot, there, target, head, kind):
        return pltpu.make_async_remote_copy(
            src_ref=(k_ref, v_ref)[kind].at[0, :, cols(head)],
            dst_ref=kv_in.at[there, head, kind],
            send_sem=kv_send.at[slot, head, kind],
            recv_sem=kv_recv.at[there, head, kind],
            device_id={"seq": target * 2 + core},
            device_id_type=MESH,
        )

    def term_copy(slot, there, target, head):
        return pltpu.make_async_remote_copy(
            src_ref=term_out.at[slot, head],
            dst_ref=term_in.at[there, head],
            send_sem=term_send.at[slot, head],
            recv_sem=term_recv.at[there, head],
            device_id={"seq": target * 2 + core},
            device_id_type=MESH,
        )

    barrier = pltpu.get_barrier_semaphore()
    for target, exists, _ in near:
        when(exists, lambda target=target: pl.semaphore_signal(
            barrier, inc=1, device_id={"seq": target * 2 + core}, device_id_type=MESH))
    pl.semaphore_wait(
        barrier, sum(1 if e is None else jnp.where(e, 1, 0).astype(jnp.int32) for _, e, _ in near)
    )

    @pl.loop(0, heads)
    def _(head):
        for slot, (target, exists, there) in enumerate(near):
            def go(slot=slot, target=target, there=there):
                for kind in range(2):
                    kv_copy(slot, there, target, head, kind).start()
            when(exists, go)

    for slot, (target, exists, there) in enumerate(near):
        if exists is not None:
            @pl.when(jnp.logical_not(exists))
            def _(slot=slot):
                @pl.loop(0, heads)
                def _(head):
                    kv_in[slot, head] = jnp.zeros(kv_in.shape[2:], kv_in.dtype)
                    term_in[slot, head] = jnp.zeros(term_in.shape[2:], term_in.dtype)

    listed = [lists_ref[tile, j] for j in range(lists_ref.shape[1])]

    def bias_of(target, exists):
        found = listed[0] == target
        for entry in listed[1:]:
            found = found | (entry == target)
        if exists is not None:
            found = found & exists
        return jnp.where(found, jnp.float32(0), jnp.float32(-jnp.inf))

    biases = [bias_of(tile, None)] + [bias_of(target, exists) for target, exists, _ in near]

    @pl.loop(0, heads)
    def _(head):
        for slot, (target, exists, _) in enumerate(near):
            def arrived(slot=slot, target=target):
                for kind in range(2):
                    kv_copy(slot, slot, target, head, kind).wait_recv()
            when(exists, arrived)

        here = cols(head)
        query = q_ref[0, :, here]
        grad = g_ref[0, :, here]

        def keys(block):
            return k_ref[0, :, here] if block == 0 else kv_in[block - 1, head, 0]

        def values(block):
            return v_ref[0, :, here] if block == 0 else kv_in[block - 1, head, 1]

        blocks = range(len(near) + 1)
        top = None
        for block in blocks:
            scores = dot(keys(block), query, 1, 1) * scale
            probs[block] = scores
            block_top = jnp.max(scores, axis=0, keepdims=True) + biases[block]
            top = block_top if top is None else jnp.maximum(top, block_top)
        total = jnp.zeros_like(top)
        for block in blocks:
            powers = jnp.exp(probs[block] - (top - biases[block]))
            probs[block] = powers
            total = total + jnp.sum(powers, axis=0, keepdims=True)
        share = 1.0 / total
        mixed = jnp.zeros((HD, query.shape[0]), jnp.float32)
        for block in blocks:
            chance = probs[block] * share
            probs[block] = chance
            mixed = mixed + dot(values(block), chance.astype(jnp.bfloat16), 0, 0)
        mixed = mixed.astype(jnp.bfloat16).astype(jnp.float32)
        o_ref[0, :, here] = mixed.T.astype(jnp.bfloat16)
        delta = jnp.sum(grad.astype(jnp.float32).T * mixed, axis=0, keepdims=True)
        query_sum = jnp.zeros((HD, query.shape[0]), jnp.float32)
        for block in list(blocks)[1:] + [0]:
            chance = probs[block]
            pressure = dot(values(block), grad, 1, 1)
            score_grad = (chance * (pressure - delta)).astype(jnp.bfloat16)
            value_term = dot(chance.astype(jnp.bfloat16), grad, 1, 0).astype(jnp.bfloat16)
            key_term = (scale * dot(score_grad, query, 1, 0)).astype(jnp.bfloat16)
            if block == 0:
                dk_ref[0, :, here] = key_term
                dv_ref[0, :, here] = value_term
            else:
                target, exists, there = near[block - 1]
                term_out[block - 1, head, 0] = key_term
                term_out[block - 1, head, 1] = value_term
                when(exists, lambda: term_copy(block - 1, there, target, head).start())
            query_sum = query_sum + dot(keys(block), score_grad, 0, 0)
        dq_ref[0, :, here] = (scale * query_sum).T.astype(jnp.bfloat16)

    @pl.loop(0, heads)
    def _(head):
        here = cols(head)
        for slot, (target, exists, _) in enumerate(near):
            when(exists, lambda: term_copy(slot, slot, target, head).wait_recv())
        for kind, out in enumerate((dk_ref, dv_ref)):
            sums = out[0, :, here].astype(jnp.float32)
            for slot in range(len(near)):
                sums = sums + term_in[slot, head, kind].astype(jnp.float32)
            out[0, :, here] = sums.astype(jnp.bfloat16)

    @pl.loop(0, heads)
    def _(head):
        for slot, (target, exists, there) in enumerate(near):
            def left(slot=slot, target=target, there=there):
                for kind in range(2):
                    kv_copy(slot, there, target, head, kind).wait_send()
                term_copy(slot, there, target, head).wait_send()
            when(exists, left)


def on_device(queries, key_vectors, value_vectors, out_grad, tile_lists):
    grid_w = lax.axis_size("seq") // 8
    tok, width = queries.shape[1:]
    heads = width // HD
    near = 3 if grid_w == 2 else 4
    vmem = pl.BlockSpec(memory_space=pltpu.VMEM)
    out = jax.ShapeDtypeStruct(queries.shape, jnp.bfloat16)
    slots = pltpu.VMEM((near, heads, 2, tok, HD), jnp.bfloat16)
    dma = pltpu.SemaphoreType.DMA
    return pl.pallas_call(
        functools.partial(kernel, grid_w),
        out_shape=(out,) * 4,
        in_specs=[pl.BlockSpec(memory_space=pltpu.SMEM)] + [vmem] * 4,
        out_specs=(vmem,) * 4,
        scratch_shapes=[
            slots,
            pltpu.VMEM((near + 1, tok, tok), jnp.float32),
            slots,
            slots,
            dma((near, heads, 2)),
            dma((near, heads, 2)),
            dma((near, heads)),
            dma((near, heads)),
        ],
        compiler_params=pltpu.CompilerParams(
            collective_id=0, has_side_effects=True, vmem_limit_bytes=56 * 2**20
        ),
        name="tiles",
    )(tile_lists, queries, key_vectors, value_vectors, out_grad)


def solution(mesh):
    rows = P(("groups", "seq"), None, None)
    return jax.shard_map(
        on_device,
        mesh=mesh,
        in_specs=(rows,) * 4 + (P("groups", None),),
        out_specs=(rows,) * 4,
        check_vma=False,
    )
```

```python
import functools

import jax
import jax.numpy as jnp
from jax import lax
from jax.experimental import pallas as pl
from jax.experimental.pallas import tpu as pltpu
from jax.sharding import PartitionSpec as P

HD = 128
MESH = pl.DeviceIdType.MESH


def dot(a, b, a_dim, b_dim):
    return lax.dot_general(
        a, b, (((a_dim,), (b_dim,)), ((), ())), preferred_element_type=jnp.float32
    )


def neighbours(grid_w):
    tile = lax.axis_index("seq") // 2
    bit0 = lax.rem(tile, 2)
    bit1 = lax.rem(tile // 2, 2)
    column = tile // 4
    if grid_w == 2:
        sides = [(tile + 4 - 8 * column, None, 0)]
    else:
        sides = [(tile - 4, column > 0, 1), (tile + 4, column < grid_w - 1, 0)]
    count = len(sides)
    return sides + [
        (tile + 2 - 4 * bit1, None, count),
        (tile + 1 - 2 * bit0, None, count + 1),
    ]


def when(exists, fn):
    if exists is None:
        fn()
    else:
        pl.when(exists)(fn)


def kernel(
    grid_w, lists_ref, q_hbm, k_hbm, v_hbm, g_hbm, o_ref, dq_ref, dk_ref, dv_ref,
    q_ref, k_ref, v_ref, g_ref, own_sems, kv_in, probs, term_out, term_in, kv_send, kv_recv, term_send, term_recv,
):
    me = lax.axis_index("seq")
    tile = me // 2
    core = lax.rem(me, 2)
    near = neighbours(grid_w)
    heads = q_ref.shape[2] // HD
    scale = HD ** (-0.5)

    def cols(head):
        return pl.ds(pl.multiple_of(head * HD, HD), HD)

    def kv_copy(slot, there, target, head, kind):
        return pltpu.make_async_remote_copy(
            src_ref=(k_hbm, v_hbm)[kind].at[0, :, cols(head)],
            dst_ref=kv_in.at[there, head, kind],
            send_sem=kv_send.at[slot, head, kind],
            recv_sem=kv_recv.at[there, head, kind],
            device_id={"seq": target * 2 + core},
            device_id_type=MESH,
        )

    def term_copy(slot, there, target, head):
        return pltpu.make_async_remote_copy(
            src_ref=term_out.at[slot, head],
            dst_ref=term_in.at[there, head],
            send_sem=term_send.at[slot, head],
            recv_sem=term_recv.at[there, head],
            device_id={"seq": target * 2 + core},
            device_id_type=MESH,
        )

    barrier = pltpu.get_barrier_semaphore()
    for target, exists, _ in near:
        when(exists, lambda target=target: pl.semaphore_signal(
            barrier, inc=1, device_id={"seq": target * 2 + core}, device_id_type=MESH))
    pl.semaphore_wait(
        barrier, sum(1 if e is None else jnp.where(e, 1, 0).astype(jnp.int32) for _, e, _ in near)
    )

    @pl.loop(0, heads)
    def _(head):
        for slot, (target, exists, there) in enumerate(near):
            def go(slot=slot, target=target, there=there):
                for kind in range(2):
                    kv_copy(slot, there, target, head, kind).start()
            when(exists, go)

    for slot, (target, exists, there) in enumerate(near):
        if exists is not None:
            @pl.when(jnp.logical_not(exists))
            def _(slot=slot):
                @pl.loop(0, heads)
                def _(head):
                    kv_in[slot, head] = jnp.zeros(kv_in.shape[2:], kv_in.dtype)
                    term_in[slot, head] = jnp.zeros(term_in.shape[2:], term_in.dtype)

    own = [
        pltpu.make_async_copy(source, held, own_sems.at[i])
        for i, (source, held) in enumerate(
            ((k_hbm, k_ref), (q_hbm, q_ref), (v_hbm, v_ref), (g_hbm, g_ref))
        )
    ]
    for copy in own:
        copy.start()

    listed = [lists_ref[tile, j] for j in range(lists_ref.shape[1])]

    def bias_of(target, exists):
        found = listed[0] == target
        for entry in listed[1:]:
            found = found | (entry == target)
        if exists is not None:
            found = found & exists
        return jnp.where(found, jnp.float32(0), jnp.float32(-jnp.inf))

    biases = [bias_of(tile, None)] + [bias_of(target, exists) for target, exists, _ in near]

    for copy in own:
        copy.wait()

    @pl.loop(0, heads)
    def _(head):
        for slot, (target, exists, _) in enumerate(near):
            def arrived(slot=slot, target=target):
                for kind in range(2):
                    kv_copy(slot, slot, target, head, kind).wait_recv()
            when(exists, arrived)

        here = cols(head)
        query = q_ref[0, :, here]
        grad = g_ref[0, :, here]

        def keys(block):
            return k_ref[0, :, here] if block == 0 else kv_in[block - 1, head, 0]

        def values(block):
            return v_ref[0, :, here] if block == 0 else kv_in[block - 1, head, 1]

        blocks = range(len(near) + 1)
        top = None
        for block in blocks:
            scores = dot(keys(block), query, 1, 1) * scale
            probs[block] = scores
            block_top = jnp.max(scores, axis=0, keepdims=True) + biases[block]
            top = block_top if top is None else jnp.maximum(top, block_top)
        total = jnp.zeros_like(top)
        for block in blocks:
            powers = jnp.exp(probs[block] - (top - biases[block]))
            probs[block] = powers
            total = total + jnp.sum(powers, axis=0, keepdims=True)
        share = 1.0 / total
        mixed = jnp.zeros((HD, query.shape[0]), jnp.float32)
        for block in blocks:
            chance = probs[block] * share
            probs[block] = chance
            mixed = mixed + dot(values(block), chance.astype(jnp.bfloat16), 0, 0)
        mixed = mixed.astype(jnp.bfloat16).astype(jnp.float32)
        o_ref[0, :, here] = mixed.T.astype(jnp.bfloat16)
        delta = jnp.sum(grad.astype(jnp.float32).T * mixed, axis=0, keepdims=True)
        query_sum = jnp.zeros((HD, query.shape[0]), jnp.float32)
        for block in list(blocks)[1:] + [0]:
            chance = probs[block]
            pressure = dot(values(block), grad, 1, 1)
            score_grad = (chance * (pressure - delta)).astype(jnp.bfloat16)
            value_term = dot(chance.astype(jnp.bfloat16), grad, 1, 0).astype(jnp.bfloat16)
            key_term = (scale * dot(score_grad, query, 1, 0)).astype(jnp.bfloat16)
            if block == 0:
                dk_ref[0, :, here] = key_term
                dv_ref[0, :, here] = value_term
            else:
                target, exists, there = near[block - 1]
                term_out[block - 1, head, 0] = key_term
                term_out[block - 1, head, 1] = value_term
                when(exists, lambda: term_copy(block - 1, there, target, head).start())
            query_sum = query_sum + dot(keys(block), score_grad, 0, 0)
        dq_ref[0, :, here] = (scale * query_sum).T.astype(jnp.bfloat16)

    @pl.loop(0, heads)
    def _(head):
        here = cols(head)
        for slot, (target, exists, _) in enumerate(near):
            when(exists, lambda: term_copy(slot, slot, target, head).wait_recv())
        for kind, out in enumerate((dk_ref, dv_ref)):
            sums = out[0, :, here].astype(jnp.float32)
            for slot in range(len(near)):
                sums = sums + term_in[slot, head, kind].astype(jnp.float32)
            out[0, :, here] = sums.astype(jnp.bfloat16)

    @pl.loop(0, heads)
    def _(head):
        for slot, (target, exists, there) in enumerate(near):
            def left(slot=slot, target=target, there=there):
                for kind in range(2):
                    kv_copy(slot, there, target, head, kind).wait_send()
                term_copy(slot, there, target, head).wait_send()
            when(exists, left)


def on_device(queries, key_vectors, value_vectors, out_grad, tile_lists):
    grid_w = lax.axis_size("seq") // 8
    tok, width = queries.shape[1:]
    heads = width // HD
    near = 3 if grid_w == 2 else 4
    vmem = pl.BlockSpec(memory_space=pltpu.VMEM)
    out = pltpu.VMEM(queries.shape, jnp.bfloat16)
    held = pltpu.VMEM(queries.shape, jnp.bfloat16)
    hbm = pl.BlockSpec(memory_space=pltpu.HBM)
    slots = pltpu.VMEM((near, heads, 2, tok, HD), jnp.bfloat16)
    dma = pltpu.SemaphoreType.DMA
    return pl.pallas_call(
        functools.partial(kernel, grid_w),
        out_shape=(out,) * 4,
        in_specs=[pl.BlockSpec(memory_space=pltpu.SMEM)] + [hbm] * 4,
        out_specs=(vmem,) * 4,
        scratch_shapes=[held] * 4 + [
            dma((4,)),
            slots,
            pltpu.VMEM((near + 1, tok, tok), jnp.float32),
            slots,
            slots,
            dma((near, heads, 2)),
            dma((near, heads, 2)),
            dma((near, heads)),
            dma((near, heads)),
        ],
        compiler_params=pltpu.CompilerParams(
            collective_id=0, has_side_effects=True, vmem_limit_bytes=50 * 2**20
        ),
        name="tiles",
    )(tile_lists, queries, key_vectors, value_vectors, out_grad)


def solution(mesh):
    rows = P(("groups", "seq"), None, None)
    return jax.shard_map(
        on_device,
        mesh=mesh,
        in_specs=(rows,) * 4 + (P("groups", None),),
        out_specs=(rows,) * 4,
        check_vma=False,
    )
```

```python
import functools

import jax
import jax.numpy as jnp
from jax import lax
from jax.experimental import pallas as pl
from jax.experimental.pallas import tpu as pltpu
from jax.sharding import PartitionSpec as P

HD = 128
MESH = pl.DeviceIdType.MESH


def dot(a, b, a_dim, b_dim):
    return lax.dot_general(
        a, b, (((a_dim,), (b_dim,)), ((), ())), preferred_element_type=jnp.float32
    )


def neighbours(grid_w):
    tile = lax.axis_index("seq") // 2
    bit0 = lax.rem(tile, 2)
    bit1 = lax.rem(tile // 2, 2)
    column = tile // 4
    if grid_w == 2:
        sides = [(tile + 4 - 8 * column, None, 0)]
    else:
        sides = [(tile - 4, column > 0, 1), (tile + 4, column < grid_w - 1, 0)]
    count = len(sides)
    return sides + [
        (tile + 2 - 4 * bit1, None, count),
        (tile + 1 - 2 * bit0, None, count + 1),
    ]


def when(exists, fn):
    if exists is None:
        fn()
    else:
        pl.when(exists)(fn)


def kernel(
    grid_w, lists_hbm, q_hbm, k_hbm, v_hbm, g_hbm, o_ref, dq_ref, dk_ref, dv_ref,
    lists_ref, q_ref, k_ref, v_ref, g_ref, own_sems, kv_in, probs, term_out, term_in, kv_send, kv_recv, term_send, term_recv,
):
    me = lax.axis_index("seq")
    tile = me // 2
    core = lax.rem(me, 2)
    near = neighbours(grid_w)
    heads = q_ref.shape[2] // HD
    scale = HD ** (-0.5)

    def cols(head):
        return pl.ds(pl.multiple_of(head * HD, HD), HD)

    def kv_copy(slot, there, target, head, kind):
        return pltpu.make_async_remote_copy(
            src_ref=(k_hbm, v_hbm)[kind].at[0, :, cols(head)],
            dst_ref=kv_in.at[there, head, kind],
            send_sem=kv_send.at[slot, head, kind],
            recv_sem=kv_recv.at[there, head, kind],
            device_id={"seq": target * 2 + core},
            device_id_type=MESH,
        )

    def term_copy(slot, there, target, head):
        return pltpu.make_async_remote_copy(
            src_ref=term_out.at[slot, head],
            dst_ref=term_in.at[there, head],
            send_sem=term_send.at[slot, head],
            recv_sem=term_recv.at[there, head],
            device_id={"seq": target * 2 + core},
            device_id_type=MESH,
        )

    barrier = pltpu.get_barrier_semaphore()
    for target, exists, _ in near:
        when(exists, lambda target=target: pl.semaphore_signal(
            barrier, inc=1, device_id={"seq": target * 2 + core}, device_id_type=MESH))
    pl.semaphore_wait(
        barrier, sum(1 if e is None else jnp.where(e, 1, 0).astype(jnp.int32) for _, e, _ in near)
    )

    @pl.loop(0, heads)
    def _(head):
        for slot, (target, exists, there) in enumerate(near):
            def go(slot=slot, target=target, there=there):
                for kind in range(2):
                    kv_copy(slot, there, target, head, kind).start()
            when(exists, go)

    for slot, (target, exists, there) in enumerate(near):
        if exists is not None:
            @pl.when(jnp.logical_not(exists))
            def _(slot=slot):
                @pl.loop(0, heads)
                def _(head):
                    kv_in[slot, head] = jnp.zeros(kv_in.shape[2:], kv_in.dtype)
                    term_in[slot, head] = jnp.zeros(term_in.shape[2:], term_in.dtype)

    own = [
        pltpu.make_async_copy(source, held, own_sems.at[i])
        for i, (source, held) in enumerate(
            (
                (lists_hbm, lists_ref),
                (k_hbm, k_ref),
                (q_hbm, q_ref),
                (v_hbm, v_ref),
                (g_hbm, g_ref),
            )
        )
    ]
    for copy in own:
        copy.start()

    for copy in own:
        copy.wait()

    listed = [lists_ref[tile, j] for j in range(lists_ref.shape[1])]

    def bias_of(target, exists):
        found = listed[0] == target
        for entry in listed[1:]:
            found = found | (entry == target)
        if exists is not None:
            found = found & exists
        return jnp.where(found, jnp.float32(0), jnp.float32(-jnp.inf))

    biases = [bias_of(tile, None)] + [bias_of(target, exists) for target, exists, _ in near]

    @pl.loop(0, heads)
    def _(head):
        for slot, (target, exists, _) in enumerate(near):
            def arrived(slot=slot, target=target):
                for kind in range(2):
                    kv_copy(slot, slot, target, head, kind).wait_recv()
            when(exists, arrived)

        here = cols(head)
        query = q_ref[0, :, here]
        grad = g_ref[0, :, here]

        def keys(block):
            return k_ref[0, :, here] if block == 0 else kv_in[block - 1, head, 0]

        def values(block):
            return v_ref[0, :, here] if block == 0 else kv_in[block - 1, head, 1]

        blocks = range(len(near) + 1)
        top = None
        for block in blocks:
            scores = dot(keys(block), query, 1, 1) * scale
            probs[block] = scores
            block_top = jnp.max(scores, axis=0, keepdims=True) + biases[block]
            top = block_top if top is None else jnp.maximum(top, block_top)
        total = jnp.zeros_like(top)
        for block in blocks:
            powers = jnp.exp(probs[block] - (top - biases[block]))
            probs[block] = powers
            total = total + jnp.sum(powers, axis=0, keepdims=True)
        share = 1.0 / total
        mixed = jnp.zeros((HD, query.shape[0]), jnp.float32)
        for block in blocks:
            chance = probs[block] * share
            probs[block] = chance
            mixed = mixed + dot(values(block), chance.astype(jnp.bfloat16), 0, 0)
        mixed = mixed.astype(jnp.bfloat16).astype(jnp.float32)
        o_ref[0, :, here] = mixed.T.astype(jnp.bfloat16)
        delta = jnp.sum(grad.astype(jnp.float32).T * mixed, axis=0, keepdims=True)
        query_sum = jnp.zeros((HD, query.shape[0]), jnp.float32)
        for block in list(blocks)[1:] + [0]:
            chance = probs[block]
            pressure = dot(values(block), grad, 1, 1)
            score_grad = (chance * (pressure - delta)).astype(jnp.bfloat16)
            value_term = dot(chance.astype(jnp.bfloat16), grad, 1, 0).astype(jnp.bfloat16)
            key_term = (scale * dot(score_grad, query, 1, 0)).astype(jnp.bfloat16)
            if block == 0:
                dk_ref[0, :, here] = key_term
                dv_ref[0, :, here] = value_term
            else:
                target, exists, there = near[block - 1]
                term_out[block - 1, head, 0] = key_term
                term_out[block - 1, head, 1] = value_term
                when(exists, lambda: term_copy(block - 1, there, target, head).start())
            query_sum = query_sum + dot(keys(block), score_grad, 0, 0)
        dq_ref[0, :, here] = (scale * query_sum).T.astype(jnp.bfloat16)

    @pl.loop(0, heads)
    def _(head):
        here = cols(head)
        for slot, (target, exists, _) in enumerate(near):
            when(exists, lambda: term_copy(slot, slot, target, head).wait_recv())
        for kind, out in enumerate((dk_ref, dv_ref)):
            sums = out[0, :, here].astype(jnp.float32)
            for slot in range(len(near)):
                sums = sums + term_in[slot, head, kind].astype(jnp.float32)
            out[0, :, here] = sums.astype(jnp.bfloat16)

    @pl.loop(0, heads)
    def _(head):
        for slot, (target, exists, there) in enumerate(near):
            def left(slot=slot, target=target, there=there):
                for kind in range(2):
                    kv_copy(slot, there, target, head, kind).wait_send()
                term_copy(slot, there, target, head).wait_send()
            when(exists, left)


def store(*refs):
    sems = refs[8]
    rows = refs[0].shape[1] // 2
    copies = [
        pltpu.make_async_copy(
            refs[i].at[:, pl.ds(part * rows, rows)],
            refs[4 + i].at[:, pl.ds(part * rows, rows)],
            sems.at[i, part],
        )
        for i in range(4)
        for part in range(2)
    ]
    for copy in copies:
        copy.start()
    for copy in copies:
        copy.wait()


def on_device(queries, key_vectors, value_vectors, out_grad, tile_lists):
    grid_w = lax.axis_size("seq") // 8
    tok, width = queries.shape[1:]
    heads = width // HD
    near = 3 if grid_w == 2 else 4
    vmem = pl.BlockSpec(memory_space=pltpu.VMEM)
    out = pltpu.VMEM(queries.shape, jnp.bfloat16)
    held = pltpu.VMEM(queries.shape, jnp.bfloat16)
    hbm = pl.BlockSpec(memory_space=pltpu.HBM)
    slots = pltpu.VMEM((near, heads, 2, tok, HD), jnp.bfloat16)
    dma = pltpu.SemaphoreType.DMA
    results = pl.pallas_call(
        functools.partial(kernel, grid_w),
        out_shape=(out,) * 4,
        in_specs=[hbm] * 5,
        out_specs=(vmem,) * 4,
        scratch_shapes=[pltpu.SMEM(tile_lists.shape, jnp.int32)] + [held] * 4 + [
            dma((5,)),
            slots,
            pltpu.VMEM((near + 1, tok, tok), jnp.float32),
            slots,
            slots,
            dma((near, heads, 2)),
            dma((near, heads, 2)),
            dma((near, heads)),
            dma((near, heads)),
        ],
        compiler_params=pltpu.CompilerParams(
            collective_id=0, has_side_effects=True, vmem_limit_bytes=42 * 2**20
        ),
        name="tiles",
    )(*[
        pltpu.with_memory_space_constraint(a, pltpu.HBM)
        for a in (tile_lists, queries, key_vectors, value_vectors, out_grad)
    ])
    return pl.pallas_call(
        store,
        out_shape=(jax.ShapeDtypeStruct(queries.shape, jnp.bfloat16),) * 4,
        in_specs=[vmem] * 4,
        out_specs=(hbm,) * 4,
        scratch_shapes=[dma((4, 2))],
        compiler_params=pltpu.CompilerParams(vmem_limit_bytes=8 * 2**20),
        name="store",
    )(*[pltpu.with_memory_space_constraint(r, pltpu.VMEM) for r in results])


def solution(mesh):
    rows = P(("groups", "seq"), None, None)
    return jax.shard_map(
        on_device,
        mesh=mesh,
        in_specs=(rows,) * 4 + (P("groups", None),),
        out_specs=(rows,) * 4,
        check_vma=False,
    )
```

```python
import functools

import jax
import jax.numpy as jnp
from jax import lax
from jax.experimental import pallas as pl
from jax.experimental.pallas import tpu as pltpu
from jax.sharding import PartitionSpec as P

HD = 128
MESH = pl.DeviceIdType.MESH


def dot(a, b, a_dim, b_dim):
    return lax.dot_general(
        a, b, (((a_dim,), (b_dim,)), ((), ())), preferred_element_type=jnp.float32
    )


def neighbours(grid_w):
    tile = lax.axis_index("seq") // 2
    bit0 = lax.rem(tile, 2)
    bit1 = lax.rem(tile // 2, 2)
    column = tile // 4
    if grid_w == 2:
        sides = [(tile + 4 - 8 * column, None, 0)]
    else:
        sides = [(tile - 4, column > 0, 1), (tile + 4, column < grid_w - 1, 0)]
    count = len(sides)
    return sides + [
        (tile + 2 - 4 * bit1, None, count),
        (tile + 1 - 2 * bit0, None, count + 1),
    ]


def when(exists, fn):
    if exists is None:
        fn()
    else:
        pl.when(exists)(fn)


def kernel(
    grid_w, lists_hbm, q_hbm, k_hbm, v_hbm, g_hbm, o_ref, dq_ref, dk_ref, dv_ref,
    lists_ref, q_ref, k_ref, v_ref, g_ref, own_sems, kv_in, probs, term_out, term_in, kv_send, kv_recv, term_send, term_recv,
):
    me = lax.axis_index("seq")
    tile = me // 2
    core = lax.rem(me, 2)
    near = neighbours(grid_w)
    heads = q_ref.shape[2] // HD
    scale = HD ** (-0.5)

    def cols(head):
        return pl.ds(pl.multiple_of(head * HD, HD), HD)

    def kv_copy(slot, there, target, head, kind):
        return pltpu.make_async_remote_copy(
            src_ref=(k_hbm, v_hbm)[kind].at[0, :, cols(head)],
            dst_ref=kv_in.at[there, head, kind],
            send_sem=kv_send.at[slot, head, kind],
            recv_sem=kv_recv.at[there, head, kind],
            device_id={"seq": target * 2 + core},
            device_id_type=MESH,
        )

    def term_copy(slot, there, target, head):
        return pltpu.make_async_remote_copy(
            src_ref=term_out.at[slot, head],
            dst_ref=term_in.at[there, head],
            send_sem=term_send.at[slot, head],
            recv_sem=term_recv.at[there, head],
            device_id={"seq": target * 2 + core},
            device_id_type=MESH,
        )

    barrier = pltpu.get_barrier_semaphore()
    for target, exists, _ in near:
        when(exists, lambda target=target: pl.semaphore_signal(
            barrier, inc=1, device_id={"seq": target * 2 + core}, device_id_type=MESH))
    pl.semaphore_wait(
        barrier, sum(1 if e is None else jnp.where(e, 1, 0).astype(jnp.int32) for _, e, _ in near)
    )

    @pl.loop(0, heads)
    def _(head):
        for slot, (target, exists, there) in enumerate(near):
            def go(slot=slot, target=target, there=there):
                for kind in range(2):
                    kv_copy(slot, there, target, head, kind).start()
            when(exists, go)

    for slot, (target, exists, there) in enumerate(near):
        if exists is not None:
            @pl.when(jnp.logical_not(exists))
            def _(slot=slot):
                @pl.loop(0, heads)
                def _(head):
                    kv_in[slot, head] = jnp.zeros(kv_in.shape[2:], kv_in.dtype)
                    term_in[slot, head] = jnp.zeros(term_in.shape[2:], term_in.dtype)

    own = [
        pltpu.make_async_copy(source, held, own_sems.at[i])
        for i, (source, held) in enumerate(
            (
                (lists_hbm, lists_ref),
                (k_hbm, k_ref),
                (q_hbm, q_ref),
                (v_hbm, v_ref),
                (g_hbm, g_ref),
            )
        )
    ]
    for copy in own:
        copy.start()

    for copy in own:
        copy.wait()

    listed = [lists_ref[tile, j] for j in range(lists_ref.shape[1])]

    def bias_of(target, exists):
        found = listed[0] == target
        for entry in listed[1:]:
            found = found | (entry == target)
        if exists is not None:
            found = found & exists
        return jnp.where(found, jnp.float32(0), jnp.float32(-jnp.inf))

    biases = [bias_of(tile, None)] + [bias_of(target, exists) for target, exists, _ in near]

    @pl.loop(0, heads)
    def _(head):
        for slot, (target, exists, _) in enumerate(near):
            def arrived(slot=slot, target=target):
                for kind in range(2):
                    kv_copy(slot, slot, target, head, kind).wait_recv()
            when(exists, arrived)

        here = cols(head)
        query = q_ref[0, :, here]
        grad = g_ref[0, :, here]

        def keys(block):
            return k_ref[0, :, here] if block == 0 else kv_in[block - 1, head, 0]

        def values(block):
            return v_ref[0, :, here] if block == 0 else kv_in[block - 1, head, 1]

        blocks = range(len(near) + 1)
        top = None
        for block in blocks:
            scores = dot(keys(block), query, 1, 1) * scale
            probs[block] = scores
            block_top = jnp.max(scores, axis=0, keepdims=True) + biases[block]
            top = block_top if top is None else jnp.maximum(top, block_top)
        total = jnp.zeros_like(top)
        for block in blocks:
            powers = jnp.exp(probs[block] - (top - biases[block]))
            probs[block] = powers
            total = total + jnp.sum(powers, axis=0, keepdims=True)
        share = 1.0 / total
        mixed = jnp.zeros((HD, query.shape[0]), jnp.float32)
        for block in blocks:
            chance = probs[block] * share
            probs[block] = chance
            mixed = mixed + dot(values(block), chance.astype(jnp.bfloat16), 0, 0)
        mixed = mixed.astype(jnp.bfloat16).astype(jnp.float32)
        o_ref[0, :, here] = mixed.T.astype(jnp.bfloat16)
        delta = jnp.sum(grad.astype(jnp.float32).T * mixed, axis=0, keepdims=True)
        query_sum = jnp.zeros((HD, query.shape[0]), jnp.float32)
        for block in list(blocks)[1:] + [0]:
            chance = probs[block]
            pressure = dot(values(block), grad, 1, 1)
            score_grad = (chance * (pressure - delta)).astype(jnp.bfloat16)
            value_term = dot(chance.astype(jnp.bfloat16), grad, 1, 0).astype(jnp.bfloat16)
            key_term = (scale * dot(score_grad, query, 1, 0)).astype(jnp.bfloat16)
            if block == 0:
                dk_ref[0, :, here] = key_term
                dv_ref[0, :, here] = value_term
            else:
                target, exists, there = near[block - 1]
                term_out[block - 1, head, 0] = key_term
                term_out[block - 1, head, 1] = value_term
                when(exists, lambda: term_copy(block - 1, there, target, head).start())
            query_sum = query_sum + dot(keys(block), score_grad, 0, 0)
        dq_ref[0, :, here] = (scale * query_sum).T.astype(jnp.bfloat16)

    @pl.loop(0, heads)
    def _(head):
        here = cols(head)
        for slot, (target, exists, _) in enumerate(near):
            when(exists, lambda: term_copy(slot, slot, target, head).wait_recv())
        for kind, out in enumerate((dk_ref, dv_ref)):
            sums = out[0, :, here].astype(jnp.float32)
            for slot in range(len(near)):
                sums = sums + term_in[slot, head, kind].astype(jnp.float32)
            out[0, :, here] = sums.astype(jnp.bfloat16)

    @pl.loop(0, heads)
    def _(head):
        for slot, (target, exists, there) in enumerate(near):
            def left(slot=slot, target=target, there=there):
                for kind in range(2):
                    kv_copy(slot, there, target, head, kind).wait_send()
                term_copy(slot, there, target, head).wait_send()
            when(exists, left)


def store(*refs):
    sems = refs[8]
    rows = refs[0].shape[1] // 6
    copies = [
        pltpu.make_async_copy(
            refs[i].at[:, pl.ds(part * rows, rows)],
            refs[4 + i].at[:, pl.ds(part * rows, rows)],
            sems.at[i, part],
        )
        for i in range(4)
        for part in range(6)
    ]
    for copy in copies:
        copy.start()
    for copy in copies:
        copy.wait()


def on_device(queries, key_vectors, value_vectors, out_grad, tile_lists):
    grid_w = lax.axis_size("seq") // 8
    tok, width = queries.shape[1:]
    heads = width // HD
    near = 3 if grid_w == 2 else 4
    vmem = pl.BlockSpec(memory_space=pltpu.VMEM)
    out = pltpu.VMEM(queries.shape, jnp.bfloat16)
    held = pltpu.VMEM(queries.shape, jnp.bfloat16)
    hbm = pl.BlockSpec(memory_space=pltpu.HBM)
    slots = pltpu.VMEM((near, heads, 2, tok, HD), jnp.bfloat16)
    dma = pltpu.SemaphoreType.DMA
    results = pl.pallas_call(
        functools.partial(kernel, grid_w),
        out_shape=(out,) * 4,
        in_specs=[hbm] * 5,
        out_specs=(vmem,) * 4,
        scratch_shapes=[pltpu.SMEM(tile_lists.shape, jnp.int32)] + [held] * 4 + [
            dma((5,)),
            slots,
            pltpu.VMEM((near + 1, tok, tok), jnp.float32),
            slots,
            slots,
            dma((near, heads, 2)),
            dma((near, heads, 2)),
            dma((near, heads)),
            dma((near, heads)),
        ],
        compiler_params=pltpu.CompilerParams(
            collective_id=0, has_side_effects=True, vmem_limit_bytes=42 * 2**20
        ),
        name="tiles",
    )(*[
        pltpu.with_memory_space_constraint(a, pltpu.HBM)
        for a in (tile_lists, queries, key_vectors, value_vectors, out_grad)
    ])
    return pl.pallas_call(
        store,
        out_shape=(jax.ShapeDtypeStruct(queries.shape, jnp.bfloat16),) * 4,
        in_specs=[vmem] * 4,
        out_specs=(hbm,) * 4,
        scratch_shapes=[dma((4, 6))],
        compiler_params=pltpu.CompilerParams(vmem_limit_bytes=8 * 2**20),
        name="store",
    )(*[pltpu.with_memory_space_constraint(r, pltpu.VMEM) for r in results])


def solution(mesh):
    rows = P(("groups", "seq"), None, None)
    return jax.shard_map(
        on_device,
        mesh=mesh,
        in_specs=(rows,) * 4 + (P("groups", None),),
        out_specs=(rows,) * 4,
        check_vma=False,
    )
```
